32 devices in a mesh: dp: 8 (over z, x), tensor: 4 (over y, core).
Axes of the slice: x: 2, y: 2, z: 4, core: 2. Of those that a mesh axis runs over, the one named last changes fastest.
Arguments:
- tokens: bfloat16 [4096, 768], P('dp', 'tensor'), may hold values from -6 to 6
- lengths: int32 [8, 4], P('dp'), may hold values from 1 to 256, 512 in all within a row
- ln1_gain: float32 [768], replicated, may hold values from 0.1 to 1.9
- ln1_bias: float32 [768], replicated, may hold values from -4 to 4
- qkv_weight: bfloat16 [3, 768, 768], P(None, None, 'tensor'), may hold values from -0.21875 to 0.21875
- qv_bias: float32 [2, 768], P(None, 'tensor'), may hold values from -4 to 4
- proj_weight: bfloat16 [768, 768], P('tensor'), may hold values from -0.75 to 0.75
- proj_bias: float32 [768], replicated, may hold values from -4 to 4
- ln2_gain: float32 [768], replicated, may hold values from 0.1 to 1.9
- ln2_bias: float32 [768], replicated, may hold values from -4 to 4
- fc_weight: bfloat16 [768, 3072], P(None, 'tensor'), may hold values from -0.21875 to 0.21875
- fc_bias: float32 [3072], P('tensor'), may hold values from -4 to 4
- out_weight: bfloat16 [3072, 768], P('tensor'), may hold values from -0.109375 to 0.109375
- out_bias: float32 [768], replicated, may hold values from -4 to 4
- cotangent: bfloat16 [4096, 768], P('dp', 'tensor'), may hold values from -6 to 6
Outputs:
- block_out: bfloat16 [4096, 768], P('dp', 'tensor')
- grad_tokens: float32 [4096, 768], P('dp', 'tensor')
- grad_ln1_gain: float32 [768], replicated
- grad_ln1_bias: float32 [768], replicated
- grad_qkv_weight: float32 [3, 768, 768], P(None, None, 'tensor')
- grad_qv_bias: float32 [2, 768], P(None, 'tensor')
- grad_proj_weight: float32 [768, 768], P('tensor')
- grad_proj_bias: float32 [768], replicated
- grad_ln2_gain: float32 [768], replicated
- grad_ln2_bias: float32 [768], replicated
- grad_fc_weight: float32 [768, 3072], P(None, 'tensor')
- grad_fc_bias: float32 [3072], P('tensor')
- grad_out_weight: float32 [3072, 768], P('tensor')
- grad_out_bias: float32 [768], replicated
The draws below stay inside these ranges and needn't reach their ends.
Inputs may be any that keep to these rules, and one draw needn't show every extreme that they name: Each row lists the lengths of the 4 sequences on one index of dp; they sum to 512 and the longest in each row is 256.
All inputs are finite; a program needn't handle non-finite values.
Results may differ from the reference program's by a relative error of at most 0.012.
The reference program's roundings to bfloat16 on the way (of `normed_one`, `weights`, `attended`, `normed_two`, `hidden`, `pre_grad_low` and `attended_grad`) count: a program that leaves them out, or rounds other values in their place, can miss the bound.
Values may be sent and summed in bfloat16 or wider, within the bound.
No kernel may reach another device: no remote copies, remote signals or barrier semaphores. Data moves between devices by JAX's collectives and lax.ppermute only.
A program may use at most 128 MiB of HBM per device.

```python
import math
import jax
import jax.numpy as jnp
import numpy as np
from jax import lax

D = 768
HEADS = 12
HEAD_DIM = 64
FF = 3072
TOK_DEV = 512
MAXLEN = 256
SLOTS = 4
TOKENS = 4096
N_DP = 8


def level_of(own_key, shape, split, least, high):
    loudness, own = 1.0, jax.random.fold_in(own_key, 6)
    for position, blocks in split:
        heights = jnp.exp(jax.random.uniform(jax.random.fold_in(own, position), (blocks,), jnp.float32, least / len(split), high / len(split)))
        loudness = loudness * jnp.repeat(heights, shape[position] // blocks).reshape([-1 if axis == position else 1 for axis in range(len(shape))])
    return loudness


def profile(count, total, limit, lean):
    loads = [(1 << 20) // math.isqrt(rank ** lean) + 1 for rank in range(2, count + 1)]
    rest, holding = total - limit - (count - 1), [1] * (count - 1)
    while rest > 0:
        movable = [i for i in range(count - 1) if holding[i] < limit]
        pool, budget = sum([loads[i] for i in movable]), rest
        for i in movable:
            extra = min(limit - holding[i], max(1, budget * loads[i] // pool), rest)
            holding[i] = holding[i] + extra
            rest = rest - extra
    return np.array([limit] + holding)


def uneven_parts(rng, number_of, total, reach, lean):
    if number_of == 2:
        one = jax.random.randint(rng, (), max(1, total - reach), min(reach, total - 1) + 1)
        return jnp.stack([one, total - one])
    tallies = jnp.asarray(profile(number_of, total, reach, lean), jnp.int32)
    couples = (number_of - 1) // 2
    giver, sink = tallies[1:1 + 2 * couples:2], tallies[2:2 + 2 * couples:2]
    margin = jnp.minimum(giver - 1, reach - sink)
    shifted = jax.random.randint(jax.random.fold_in(rng, 1), (couples,), 0, 1 << 20) % (margin + 1)
    tallies = tallies.at[1:1 + 2 * couples:2].set(giver - shifted).at[2:2 + 2 * couples:2].set(sink + shifted)
    return tallies[jax.random.permutation(jax.random.fold_in(rng, 2), number_of)]


def scatter_about(rng, shape, width, reach, shards=(), kind=jnp.bfloat16):
    gain = level_of(rng, shape, shards, -0.22, 0.18) if shards else 1.0
    entries = jax.random.normal(rng, shape, jnp.float32) * width * gain
    return jnp.minimum(jnp.maximum(entries, -reach), reach).astype(kind)


def setup_inputs(seed: int = 0) -> dict:
    streams_of = jax.random.split(jax.random.key(seed), 16)
    return {
        "tokens": scatter_about(streams_of[0], (TOKENS, D), 1.0, 6.0, ((0, 8), (1, 4))),
        "lengths": jax.vmap(lambda own: uneven_parts(own, SLOTS, TOK_DEV, MAXLEN, 2))(jax.random.split(streams_of[1], N_DP)).reshape((N_DP, SLOTS)).astype(jnp.int32),
        "ln1_gain": jnp.clip(1.0 + 0.18 * jax.random.normal(streams_of[2], (D,), jnp.float32), 0.1, 1.9),
        "ln1_bias": scatter_about(streams_of[3], (D,), 0.3, 4.0, (), jnp.float32),
        "qkv_weight": scatter_about(streams_of[4], (3, D, D), D ** -0.5, 0.21875, ((2, 4),)),
        "qv_bias": scatter_about(streams_of[5], (2, D), 0.5, 4.0, ((1, 4),), jnp.float32),
        "proj_weight": scatter_about(streams_of[6], (D, D), 64 ** -0.5, 0.75, ((0, 4),)),
        "proj_bias": scatter_about(streams_of[7], (D,), 0.5, 4.0, (), jnp.float32),
        "ln2_gain": jnp.clip(1.0 + 0.18 * jax.random.normal(streams_of[8], (D,), jnp.float32), 0.1, 1.9),
        "ln2_bias": scatter_about(streams_of[9], (D,), 0.3, 4.0, (), jnp.float32),
        "fc_weight": scatter_about(streams_of[10], (D, FF), D ** -0.5, 0.21875, ((1, 4),)),
        "fc_bias": scatter_about(streams_of[11], (FF,), 0.5, 4.0, ((0, 4),), jnp.float32),
        "out_weight": scatter_about(streams_of[12], (FF, D), FF ** -0.5, 0.109375, ((0, 4),)),
        "out_bias": scatter_about(streams_of[13], (D,), 0.5, 4.0, (), jnp.float32),
        "cotangent": scatter_about(streams_of[14], (TOKENS, D), 1.0, 6.0, ((0, 8), (1, 4))),
    }


EPSILON = 1e-05
MASKED = -1e+30

def layer_norm(values, gain_vec, bias_vec):
    average = lax.optimization_barrier(jnp.mean(values, axis=-1, keepdims=True))
    centred = values - average
    variance = lax.optimization_barrier(jnp.mean(centred * centred, axis=-1, keepdims=True))
    return centred * lax.rsqrt(variance + EPSILON) * gain_vec + bias_vec

def gelu_tanh(values):
    return 0.5 * values * (1.0 + jnp.tanh(0.7978845608028654 * (values + 0.044715 * values * values * values)))

def product(pattern, first_op, second_op):
    return jnp.einsum(pattern, first_op.astype(jnp.float32), second_op.astype(jnp.float32))

def segment_ids(seq_lengths, row_count):
    seq_ends = jnp.cumsum(seq_lengths).astype(jnp.int32)
    positions = jnp.arange(row_count, dtype=jnp.int32)
    return lax.optimization_barrier(jnp.sum((positions[:, None] >= seq_ends[None, :]).astype(jnp.int32), axis=1)).astype(jnp.int32)

def allowed_block(segments, offset, block_rows):
    positions = jnp.arange(segments.shape[0], dtype=jnp.int32)
    same_seq = segments[offset:offset + block_rows, None] == segments[None, :]
    causal = positions[offset:offset + block_rows, None] >= positions[None, :]
    return (same_seq & causal)[None]

def attend(queries, key_heads, values, segments, score_scale):
    row_count = queries.shape[0]
    block_rows = min(512, row_count)
    outputs = []
    totals = []
    for offset in range(0, row_count, block_rows):
        allowed = allowed_block(segments, offset, block_rows)
        scores = product('qhd,khd->hqk', queries[offset:offset + block_rows], key_heads) * score_scale
        scores = jnp.where(allowed, scores, MASKED)
        highest = lax.optimization_barrier(jnp.max(scores, axis=-1, keepdims=True))
        log_total = highest + jnp.log(lax.optimization_barrier(jnp.sum(jnp.exp(scores - highest), axis=-1, keepdims=True)))
        weights = jnp.exp(scores - log_total).astype(jnp.bfloat16)
        outputs.append(product('hqk,khd->qhd', weights, values).astype(jnp.bfloat16))
        totals.append(log_total)
    return (jnp.concatenate(outputs, axis=0), jnp.concatenate(totals, axis=1))

def attend_back(queries, key_heads, values, attended, log_totals, out_grads, segments, score_scale):
    row_count = queries.shape[0]
    block_rows = min(512, row_count)
    row_dots = lax.optimization_barrier(jnp.sum(out_grads.astype(jnp.float32) * attended.astype(jnp.float32), axis=-1)).T[:, :, None]
    key_grads = jnp.zeros(key_heads.shape, jnp.float32)
    value_grads = jnp.zeros(values.shape, jnp.float32)
    query_grads = []
    for offset in range(0, row_count, block_rows):
        finish = offset + block_rows
        allowed = allowed_block(segments, offset, block_rows)
        block_queries = queries[offset:finish]
        block_grads = out_grads[offset:finish]
        scores = product('qhd,khd->hqk', block_queries, key_heads) * score_scale
        scores = jnp.where(allowed, scores, MASKED)
        weights = jnp.exp(scores - log_totals[:, offset:finish])
        value_grads = value_grads + product('hqk,qhd->khd', weights.astype(jnp.bfloat16), block_grads)
        weight_grads = product('qhd,khd->hqk', block_grads, values)
        score_grads = (weights * (weight_grads - row_dots[:, offset:finish]) * score_scale).astype(jnp.bfloat16)
        query_grads.append(product('hqk,khd->qhd', score_grads, key_heads).astype(jnp.bfloat16))
        key_grads = key_grads + product('hqk,qhd->khd', score_grads, block_queries)
    return (jnp.concatenate(query_grads, axis=0), key_grads.astype(jnp.bfloat16), value_grads.astype(jnp.bfloat16))

def layer_pass(tokens, seq_lengths, cotangent, params):
    ln1_gain, ln1_bias, qkv_weight, qv_bias, proj_weight, proj_bias, ln2_gain, ln2_bias, fc_weight, fc_bias, out_weight, out_bias = params
    row_count = tokens.shape[0]
    score_scale = HEAD_DIM ** (-0.5)
    segments = segment_ids(seq_lengths, row_count)
    residual_in = tokens.astype(jnp.float32)
    normed_one = layer_norm(residual_in, ln1_gain, ln1_bias).astype(jnp.bfloat16)
    projected = product('td,cdf->ctf', normed_one, qkv_weight)
    queries = (projected[0] + qv_bias[0]).astype(jnp.bfloat16).reshape(row_count, HEADS, HEAD_DIM)
    key_heads = projected[1].astype(jnp.bfloat16).reshape(row_count, HEADS, HEAD_DIM)
    values = (projected[2] + qv_bias[1]).astype(jnp.bfloat16).reshape(row_count, HEADS, HEAD_DIM)
    attended, log_totals = attend(queries, key_heads, values, segments, score_scale)
    flat_attended = attended.reshape(row_count, D)
    residual_mid = residual_in + jnp.dot(flat_attended, proj_weight, preferred_element_type=jnp.float32) + proj_bias
    normed_two = layer_norm(residual_mid, ln2_gain, ln2_bias).astype(jnp.bfloat16)
    pre_act = jnp.dot(normed_two, fc_weight, preferred_element_type=jnp.float32) + fc_bias
    hidden = gelu_tanh(pre_act).astype(jnp.bfloat16)
    block_out = (residual_mid + (jnp.dot(hidden, out_weight, preferred_element_type=jnp.float32) + out_bias)).astype(jnp.bfloat16)
    hidden_grad = jnp.dot(cotangent, out_weight.T, preferred_element_type=jnp.float32)
    gelu_back = jax.vjp(gelu_tanh, pre_act)[1]
    pre_grad = gelu_back(hidden_grad)[0]
    pre_grad_low = pre_grad.astype(jnp.bfloat16)
    grad_out_weight = jnp.dot(hidden.T, cotangent, preferred_element_type=jnp.float32)
    grad_out_bias = lax.optimization_barrier(jnp.sum(cotangent.astype(jnp.float32), axis=0))
    grad_fc_weight = jnp.dot(normed_two.T, pre_grad_low, preferred_element_type=jnp.float32)
    grad_fc_bias = lax.optimization_barrier(jnp.sum(pre_grad, axis=0))
    normed_two_grad = jnp.dot(pre_grad_low, fc_weight.T, preferred_element_type=jnp.float32)
    norm_two_back = jax.vjp(layer_norm, residual_mid, ln2_gain, ln2_bias)[1]
    mid_part, grad_ln2_gain, grad_ln2_bias = norm_two_back(normed_two_grad)
    mid_grad = cotangent.astype(jnp.float32) + mid_part
    mid_low = mid_grad.astype(jnp.bfloat16)
    grad_proj_weight = jnp.dot(flat_attended.T, mid_low, preferred_element_type=jnp.float32)
    grad_proj_bias = lax.optimization_barrier(jnp.sum(mid_grad, axis=0))
    attended_grad = jnp.dot(mid_low, proj_weight.T, preferred_element_type=jnp.float32).astype(jnp.bfloat16)
    attended_grad = attended_grad.reshape(row_count, HEADS, HEAD_DIM)
    query_grads, key_grads, value_grads = attend_back(queries, key_heads, values, attended, log_totals, attended_grad, segments, score_scale)
    stacked = jnp.stack([query_grads.reshape(row_count, D), key_grads.reshape(row_count, D), value_grads.reshape(row_count, D)], axis=1)
    grad_qkv_weight = product('td,tcf->cdf', normed_one, stacked)
    grad_qv_bias = jnp.stack([lax.optimization_barrier(jnp.sum(stacked[:, 0].astype(jnp.float32), axis=0)), lax.optimization_barrier(jnp.sum(stacked[:, 2].astype(jnp.float32), axis=0))])
    normed_one_grad = product('tcf,cdf->td', stacked, qkv_weight)
    norm_one_back = jax.vjp(layer_norm, residual_in, ln1_gain, ln1_bias)[1]
    in_part, grad_ln1_gain, grad_ln1_bias = norm_one_back(normed_one_grad)
    input_grad = mid_grad + in_part
    grads = (grad_ln1_gain, grad_ln1_bias, grad_qkv_weight, grad_qv_bias, grad_proj_weight, grad_proj_bias, grad_ln2_gain, grad_ln2_bias, grad_fc_weight, grad_fc_bias, grad_out_weight, grad_out_bias)
    return (block_out, input_grad, grads)

def reference(tokens, lengths, ln1_gain, ln1_bias, qkv_weight, qv_bias, proj_weight, proj_bias, ln2_gain, ln2_bias, fc_weight, fc_bias, out_weight, out_bias, cotangent):
    params = (ln1_gain, ln1_bias, qkv_weight, qv_bias, proj_weight, proj_bias, ln2_gain, ln2_bias, fc_weight, fc_bias, out_weight, out_bias)

    def visit(carry, inputs):
        block_tokens, seq_lengths, block_cot = inputs
        block_out, input_grad, grads = layer_pass(block_tokens, seq_lengths, block_cot, params)
        summed = tuple((running + current for running, current in zip(carry, grads)))
        return (summed, (block_out, input_grad))
    start_grads = tuple((jnp.zeros(param.shape, jnp.float32) for param in params))
    totals, (outputs, input_grads) = lax.scan(visit, start_grads, (tokens.reshape(N_DP, TOK_DEV, D), lengths, cotangent.reshape(N_DP, TOK_DEV, D)))
    return (outputs.reshape(TOKENS, D), input_grads.reshape(TOKENS, D), totals[0], totals[1], totals[2], totals[3], totals[4], totals[5], totals[6], totals[7], totals[8], totals[9], totals[10], totals[11])
```

```python
import jax
import jax.numpy as jnp
from jax import lax
from jax.sharding import PartitionSpec as P

HEAD_DIM = 64
EPSILON = 1e-05
MASKED = -1e30

WIRE = jnp.bfloat16
WIDE = jnp.float32


def bit_count(size):
    return size.bit_length() - 1


def bit_of(axis, bit):
    return (lax.axis_index(axis) >> bit) & 1


def swap(value, axis, size, bit):
    return lax.ppermute(value, axis, [(i, i ^ (1 << bit)) for i in range(size)])


def reduce_scatter(part, axis, size, order):
    bits = bit_count(size)
    left = list(range(bits - 1, -1, -1))
    block = part.reshape((2,) * bits + (part.shape[0] // size,) + part.shape[1:])
    for bit in order:
        place = left.index(bit)
        mine = bit_of(axis, bit)
        send = lax.dynamic_index_in_dim(block, 1 - mine, place, False).astype(WIRE)
        keep = lax.dynamic_index_in_dim(block, mine, place, False)
        block = keep.astype(WIDE) + swap(send, axis, size, bit).astype(WIDE)
        left.remove(bit)
    return block


def all_gather(own, axis, size, order):
    held = []
    block = own
    for bit in reversed(order):
        held.append(bit)
        held.sort(reverse=True)
        place = held.index(bit)
        mine = bit_of(axis, bit)
        other = swap(block, axis, size, bit)
        first = jnp.where(mine == 1, other, block)
        second = jnp.where(mine == 1, block, other)
        block = jnp.stack([first, second], axis=place)
    return block.reshape((size * own.shape[0],) + own.shape[1:])


def all_sum(value, axis, size):
    for bit in range(bit_count(size)):
        value = value + swap(value, axis, size, bit)
    return value


def layer_norm(values, gain_vec, bias_vec):
    average = jnp.mean(values, axis=0, keepdims=True)
    centred = values - average
    variance = jnp.mean(centred * centred, axis=0, keepdims=True)
    return centred * lax.rsqrt(variance + EPSILON) * gain_vec[:, None] + bias_vec[:, None]


def gelu_tanh(values):
    return (
        0.5
        * values
        * (1.0 + jnp.tanh(0.7978845608028654 * (values + 0.044715 * values * values * values)))
    )


def product(pattern, first_op, second_op):
    return jnp.einsum(pattern, first_op, second_op, preferred_element_type=WIDE)


def make_local(dp_size, tensor_size):
    tensor_order = list(range(bit_count(tensor_size)))
    dp_order = list(range(bit_count(dp_size)))
    dp_other = dp_order[1:] + dp_order[:1]

    def scatter_tensor(part):
        return reduce_scatter(part, "tensor", tensor_size, tensor_order)

    def gather_tensor(own):
        return all_gather(own, "tensor", tensor_size, tensor_order)

    def sum_dp(grad, order):
        own = reduce_scatter(grad, "dp", dp_size, order).astype(WIRE)
        return all_gather(own, "dp", dp_size, order).astype(WIDE)

    def local(
        tokens,
        lengths,
        ln1_gain,
        ln1_bias,
        qkv_weight,
        qv_bias,
        proj_weight,
        proj_bias,
        ln2_gain,
        ln2_bias,
        fc_weight,
        fc_bias,
        out_weight,
        out_bias,
        cotangent,
    ):
        row_count = tokens.shape[0]
        width = proj_weight.shape[1]
        own_width = proj_weight.shape[0]
        heads = own_width // HEAD_DIM
        scale = HEAD_DIM ** (-0.5)
        start = lax.axis_index("tensor") * own_width
        seq_ends = jnp.cumsum(lengths[0])
        positions = jnp.arange(row_count, dtype=jnp.int32)
        segments = jnp.sum((positions[:, None] >= seq_ends[None, :]).astype(jnp.int32), axis=1)
        allowed = (segments[:, None] == segments[None, :]) & (
            positions[:, None] <= positions[None, :]
        )
        qkv_t = jnp.swapaxes(qkv_weight, 1, 2).reshape(3 * own_width, width)
        residual_in = gather_tensor(tokens.T).astype(WIDE)
        normed_one = layer_norm(residual_in, ln1_gain, ln1_bias).astype(jnp.bfloat16)
        projected = product("fd,dt->ft", qkv_t, normed_one).reshape(3, own_width, row_count)
        queries = (projected[0] + qv_bias[0][:, None]).astype(jnp.bfloat16)
        key_heads = projected[1].astype(jnp.bfloat16)
        values = (projected[2] + qv_bias[1][:, None]).astype(jnp.bfloat16)
        queries = queries.reshape(heads, HEAD_DIM, row_count)
        key_heads = key_heads.reshape(heads, HEAD_DIM, row_count)
        values = values.reshape(heads, HEAD_DIM, row_count)
        scores = jnp.where(allowed, product("hek,heq->hkq", key_heads, queries) * scale, MASKED)
        highest = jnp.max(scores, axis=1, keepdims=True)
        log_total = highest + jnp.log(jnp.sum(jnp.exp(scores - highest), axis=1, keepdims=True))
        probs = jnp.exp(scores - log_total)
        probs_low = probs.astype(jnp.bfloat16)
        attended = product("hek,hkq->heq", values, probs_low).astype(jnp.bfloat16)
        flat_attended = attended.reshape(own_width, row_count)
        mixed = gather_tensor(
            scatter_tensor(product("fd,ft->dt", proj_weight, flat_attended)).astype(WIRE)
        )
        residual_mid = residual_in + mixed.astype(WIDE) + proj_bias[:, None]
        normed_two = layer_norm(residual_mid, ln2_gain, ln2_bias).astype(jnp.bfloat16)
        mid_share = lax.dynamic_slice_in_dim(residual_mid, start, own_width, 0)
        pre_act = product("dh,dt->ht", fc_weight, normed_two) + fc_bias[:, None]
        hidden = gelu_tanh(pre_act).astype(jnp.bfloat16)
        out_grad = gather_tensor(cotangent.T)
        out_grad_wide = out_grad.astype(WIDE)
        hidden_grad = product("hd,dt->ht", out_weight, out_grad)
        pre_grad = jax.vjp(gelu_tanh, pre_act)[1](hidden_grad)[0]
        pre_grad_low = pre_grad.astype(jnp.bfloat16)
        two_part = product("dh,ht->dt", fc_weight, pre_grad_low)
        normed_two_grad = gather_tensor(scatter_tensor(two_part).astype(WIRE)).astype(WIDE)
        grad_out_weight = sum_dp(product("ht,dt->hd", hidden, out_grad), dp_order)
        grad_fc_weight = sum_dp(product("dt,ht->dh", normed_two, pre_grad_low), dp_order)
        mlp_share = scatter_tensor(product("hd,ht->dt", out_weight, hidden))
        bias_share = lax.dynamic_slice_in_dim(out_bias, start, own_width, 0)
        block_out = (mid_share + (mlp_share + bias_share[:, None])).astype(jnp.bfloat16)
        grad_out_bias = jnp.sum(out_grad_wide, axis=1)
        grad_fc_bias = jnp.sum(pre_grad, axis=1)
        mid_part, grad_ln2_gain, grad_ln2_bias = jax.vjp(
            layer_norm, residual_mid, ln2_gain, ln2_bias
        )[1](normed_two_grad)
        mid_grad = out_grad_wide + mid_part
        mid_low = mid_grad.astype(jnp.bfloat16)
        grad_proj_bias = jnp.sum(mid_grad, axis=1)
        grad_proj_weight = product("ft,dt->fd", flat_attended, mid_low)
        attended_grad = product("fd,dt->ft", proj_weight, mid_low).astype(jnp.bfloat16)
        attended_grad = attended_grad.reshape(heads, HEAD_DIM, row_count)
        row_dots = jnp.sum(
            attended_grad.astype(WIDE) * attended.astype(WIDE), axis=1, keepdims=True
        )
        value_grads = product("hkq,heq->hek", probs_low, attended_grad).astype(jnp.bfloat16)
        weight_grads = product("hek,heq->hkq", values, attended_grad)
        score_grads = (probs * (weight_grads - row_dots) * scale).astype(jnp.bfloat16)
        query_grads = product("hek,hkq->heq", key_heads, score_grads).astype(jnp.bfloat16)
        key_grads = product("heq,hkq->hek", queries, score_grads).astype(jnp.bfloat16)
        stacked = jnp.concatenate([query_grads, key_grads, value_grads]).reshape(
            3 * own_width, row_count
        )
        grad_qkv = product("ft,dt->fd", stacked, normed_one)
        sums = jnp.sum(stacked.astype(WIDE), axis=1)
        grad_qv_bias = jnp.concatenate([sums[:own_width], sums[2 * own_width :]])
        one_part = product("fd,ft->dt", qkv_t, stacked)
        average = jnp.mean(residual_in, axis=0, keepdims=True)
        centred = residual_in - average
        inverse = lax.rsqrt(jnp.mean(centred * centred, axis=0, keepdims=True) + EPSILON)
        unit = centred * inverse
        scaled = one_part * ln1_gain[:, None]
        linear = jnp.concatenate(
            [
                jnp.sum(scaled, axis=0),
                jnp.sum(scaled * unit, axis=0),
                jnp.sum(one_part * unit, axis=1),
                jnp.sum(one_part, axis=1),
            ]
        )
        linear = all_sum(linear, "tensor", tensor_size)
        row_sum = linear[:row_count][None] / width
        row_dot = linear[row_count : 2 * row_count][None] / width
        grad_ln1 = linear[2 * row_count :]
        share = scatter_tensor(one_part)
        unit_share = lax.dynamic_slice_in_dim(unit, start, own_width, 0)
        gain_share = lax.dynamic_slice_in_dim(ln1_gain, start, own_width, 0)
        mid_grad_share = lax.dynamic_slice_in_dim(mid_grad, start, own_width, 0)
        in_part = inverse * (share * gain_share[:, None] - row_sum - unit_share * row_dot)
        grad_tokens = mid_grad_share + in_part
        small = jnp.concatenate(
            [
                grad_fc_bias,
                grad_out_bias,
                grad_ln2_gain,
                grad_ln2_bias,
                grad_proj_bias,
                grad_qv_bias,
                grad_ln1,
            ]
        )
        small = all_sum(small, "dp", dp_size)
        cuts = []
        place = 0
        for length in (fc_bias.shape[0], width, width, width, width, 2 * own_width, width, width):
            cuts.append(small[place : place + length])
            place += length
        attn = jnp.concatenate([grad_qkv, grad_proj_weight])
        half = width // 2
        attn = jnp.concatenate(
            [sum_dp(attn[:, :half], dp_order), sum_dp(attn[:, half:], dp_other)], axis=1
        )
        grad_qkv_weight = jnp.swapaxes(
            attn[: 3 * own_width].reshape(3, own_width, width), 1, 2
        )
        return (
            block_out.T,
            grad_tokens.T,
            cuts[6],
            cuts[7],
            grad_qkv_weight,
            cuts[5].reshape(2, own_width),
            attn[3 * own_width :],
            cuts[4],
            cuts[2],
            cuts[3],
            grad_fc_weight,
            cuts[0],
            grad_out_weight,
            cuts[1],
        )

    return local


def solution(mesh):
    placed = (
        P("dp", "tensor"),
        P("dp", None),
        P(),
        P(),
        P(None, None, "tensor"),
        P(None, "tensor"),
        P("tensor", None),
        P(),
        P(),
        P(),
        P(None, "tensor"),
        P("tensor"),
        P("tensor", None),
        P(),
        P("dp", "tensor"),
    )
    return jax.shard_map(
        make_local(mesh.shape["dp"], mesh.shape["tensor"]),
        mesh=mesh,
        in_specs=placed,
        out_specs=(
            P("dp", "tensor"),
            P("dp", "tensor"),
            P(),
            P(),
            P(None, None, "tensor"),
            P(None, "tensor"),
            P("tensor", None),
            P(),
            P(),
            P(),
            P(None, "tensor"),
            P("tensor"),
            P("tensor", None),
            P(),
        ),
        check_vma=False,
    )
```

```python
import functools
import jax
import jax.numpy as jnp
from jax import lax
from jax.experimental import pallas as pl
from jax.experimental.pallas import tpu as pltpu
from jax.sharding import PartitionSpec as P

HEAD_DIM = 64
EPSILON = 1e-05
MASKED = -1e30
LOW = jnp.bfloat16
WIDE = jnp.float32
LANES = 128
ROOT = 0.7978845608028654
CUBE = 0.044715


def dot(first, second, first_dim, second_dim):
    return lax.dot_general(
        first, second, (((first_dim,), (second_dim,)), ((), ())), preferred_element_type=WIDE
    )


def column(row, width):
    turned = jnp.broadcast_to(row, (LANES, row.shape[1])).T
    return jnp.concatenate([turned] * (width // LANES), axis=1)


def row_sums(values):
    part = values[:, :LANES]
    for at in range(LANES, values.shape[1], LANES):
        part = part + values[:, at : at + LANES]
    return jnp.sum(part.T, axis=0, keepdims=True)


def unit_rows(values):
    count = values.shape[0]
    average = jnp.sum(values, axis=0, keepdims=True) / count
    centred = values - average
    variance = jnp.sum(centred * centred, axis=0, keepdims=True) / count
    inverse = lax.rsqrt(variance + EPSILON)
    return centred * inverse, inverse


def whole(shape, dtype):
    return jax.ShapeDtypeStruct(shape, dtype)


def call(body, outs, scratch, scalars, *args):
    spec = pl.BlockSpec(memory_space=pltpu.VMEM)
    return pl.pallas_call(
        body,
        out_shape=outs,
        in_specs=[pl.BlockSpec(memory_space=pltpu.SMEM)] * len(scalars) + [spec] * len(args),
        out_specs=[spec] * len(outs),
        scratch_shapes=scratch,
        compiler_params=pltpu.CompilerParams(vmem_limit_bytes=56 * 1024 * 1024),
    )(*scalars, *args)


def split_tensor(result, core, send, keep):
    for y in range(send.shape[0]):
        send[y] = result[2 * y + 1 - core].astype(LOW)
        keep[y] = result[2 * y + core]


def make_mlp(parts):
    def body(bits, *refs):
        mixed_pieces = refs[:parts]
        cot_pieces = refs[parts : 2 * parts]
        tokens, proj_bias, gain, bias, fc_w, fc_b, out_w, out_b = refs[2 * parts : 2 * parts + 8]
        (send, keep, hidden, grad_low, normed, unit, inverse, fc_b_grad, cot, base, mixed,
         result) = refs[2 * parts + 8 :]
        assemble(bits, mixed_pieces, mixed)
        assemble(bits, cot_pieces, cot)
        rows = tokens.shape[1]
        blk = result.shape[1]
        mid = tokens[...].astype(WIDE) + flat(mixed).astype(WIDE) + column(proj_bias[...], rows)
        with_bias = mid + column(out_b[...], rows)
        for j in range(parts):
            result[j] = with_bias[j * blk : (j + 1) * blk, :]
        base[...] = result[bits[0]]
        unit_v, inverse_v = unit_rows(mid)
        unit[...] = unit_v
        inverse[...] = inverse_v
        normed[...] = (unit_v * column(gain[...], rows) + column(bias[...], rows)).astype(LOW)
        cot_v = flat(cot)
        block = 256
        for at in range(0, fc_w.shape[1], block):
            sl = slice(at, at + block)
            act = dot(fc_w[:, sl], normed[...], 0, 0) + column(fc_b[:, sl], rows)
            back = dot(out_w[sl, :], cot_v, 1, 0)
            square = act * act
            tan = jnp.tanh(ROOT * (act + CUBE * square * act))
            half = 0.5 * (1.0 + tan)
            hidden[sl, :] = (act * half).astype(LOW)
            slope = half + 0.5 * act * (1.0 - tan * tan) * (ROOT * (1.0 + 3.0 * CUBE * square))
            grad = back * slope
            grad_low[sl, :] = grad.astype(LOW)
            fc_b_grad[:, sl] = row_sums(grad)
        for j in range(parts):
            result[j] = dot(fc_w[j * blk : (j + 1) * blk, :], grad_low[...], 1, 0)
        split_tensor(result, bits[0] & 1, send, keep)

    return body


def mlp(bits, mixed, cot, tokens, proj_bias, gain, bias, fc_w, fc_b, out_w, out_b):
    parts = len(mixed)
    d, t = tokens.shape
    h = fc_w.shape[1]
    blk = d // parts
    outs = [
        whole((parts // 2, blk, t), LOW), whole((parts // 2, blk, t), WIDE),
        whole((h, t), LOW), whole((h, t), LOW), whole((d, t), LOW),
        whole((d, t), WIDE), whole((1, t), WIDE), whole((1, h), WIDE),
        whole((parts, blk, t), LOW), whole((blk, t), WIDE),
    ]
    return call(make_mlp(parts), outs,
                [pltpu.VMEM((parts, blk, t), LOW), pltpu.VMEM((parts, blk, t), WIDE)], (bits,),
                *mixed, *cot, tokens, proj_bias, gain, bias, fc_w, fc_b, out_w, out_b)


def split_half(scratch, bit, send, keep):
    send[...] = scratch[1 - bit].astype(LOW)
    keep[...] = scratch[bit]


def mlp_grad_body(bits, hidden, grad_low, normed, out_w, cot,
                  out_send, out_keep, fc_send, fc_keep, mlp_send, mlp_keep, cot_sum, square, result):
    half = square.shape[1]
    for j in range(2):
        square[j] = dot(hidden[j * half : (j + 1) * half, :], cot[...], 1, 1)
    split_half(square, bits[1] & 1, out_send, out_keep)
    for j in range(2):
        square[j] = dot(normed[j * half : (j + 1) * half, :], grad_low[...], 1, 1)
    split_half(square, (bits[1] >> 1) & 1, fc_send, fc_keep)
    cot_sum[...] = row_sums(cot[...].astype(WIDE))
    blk = result.shape[1]
    for j in range(result.shape[0]):
        result[j] = dot(out_w[:, j * blk : (j + 1) * blk], hidden[...], 0, 0)
    split_tensor(result, bits[0] & 1, mlp_send, mlp_keep)


def mlp_grad(bits, hidden, grad_low, normed, out_w, cot, parts):
    d, t = cot.shape
    h = hidden.shape[0]
    outs = [
        whole((h // 2, d), LOW), whole((h // 2, d), WIDE),
        whole((d // 2, h), LOW), whole((d // 2, h), WIDE),
        whole((parts // 2, d // parts, t), LOW), whole((parts // 2, d // parts, t), WIDE),
        whole((1, d), WIDE),
    ]
    return call(mlp_grad_body, outs,
                [pltpu.VMEM((2, h // 2, d), WIDE), pltpu.VMEM((parts, d // parts, t), WIDE)], (bits,),
                hidden, grad_low, normed, out_w, cot)


def assemble(bits, pieces, full):
    own = bits[0]
    for k, piece in enumerate(pieces):
        full[own ^ k] = piece[...]


def flat(ref):
    value = ref[...]
    return value.reshape(value.shape[0] * value.shape[1], value.shape[2])


def starts(lengths, at, size):
    token = lax.broadcasted_iota(jnp.int32, (1, size), 1) + at
    first = jnp.zeros((1, size), jnp.int32)
    end = lengths[0, 0]
    for slot in range(1, lengths.shape[1]):
        first = jnp.where(token >= end, end, first)
        end = end + lengths[0, slot]
    return first


BLOCK = 256
REACH = 256


def key_range(at):
    low = max(0, (at - REACH + 1) // LANES * LANES)
    return low, at + BLOCK


def allowed(lengths, at):
    low, high = key_range(at)
    shape = (high - low, BLOCK)
    key = lax.broadcasted_iota(jnp.int32, shape, 0) + low
    token = lax.broadcasted_iota(jnp.int32, shape, 1) + at
    return (key <= token) & (key >= starts(lengths, at, BLOCK))


def make_attend(parts):
    def body(bits, lengths, *refs):
        pieces = refs[:parts]
        gain, bias, qkv_t, qv_bias, proj_w = refs[parts : parts + 5]
        send, keep, tokens, normed, unit, inverse, qkv, attended, totals, result = refs[parts + 5 :]
        assemble(bits, pieces, tokens)
        unit_v, inverse_v = unit_rows(flat(tokens).astype(WIDE))
        rows = unit_v.shape[1]
        unit[...] = unit_v
        inverse[...] = inverse_v
        normed[...] = (unit_v * column(gain[...], rows) + column(bias[...], rows)).astype(LOW)
        width = proj_w.shape[0]
        for c in range(3):
            made = dot(qkv_t[c * width : (c + 1) * width, :], normed[...], 1, 0)
            if c != 1:
                made = made + column(qv_bias[:, c // 2 * width : (c // 2 + 1) * width], rows)
            qkv[c * width : (c + 1) * width, :] = made.astype(LOW)
        scale = HEAD_DIM ** (-0.5)
        for at in range(0, rows, BLOCK):
            low, high = key_range(at)
            mask = allowed(lengths, at)
            for head in range(width // HEAD_DIM):
                here = head * HEAD_DIM
                q = qkv[here : here + HEAD_DIM, at : at + BLOCK]
                k = qkv[width + here : width + here + HEAD_DIM, low:high]
                v = qkv[2 * width + here : 2 * width + here + HEAD_DIM, low:high]
                scores = jnp.where(mask, dot(k, q, 0, 0) * scale, MASKED)
                highest = jnp.max(scores, axis=0, keepdims=True)
                total = highest + jnp.log(jnp.sum(jnp.exp(scores - highest), axis=0, keepdims=True))
                weights = jnp.exp(scores - total).astype(LOW)
                totals[head : head + 1, at : at + BLOCK] = total
                attended[here : here + HEAD_DIM, at : at + BLOCK] = dot(v, weights, 1, 0).astype(LOW)
        blk = result.shape[1]
        for j in range(parts):
            result[j] = dot(proj_w[:, j * blk : (j + 1) * blk], attended[...], 0, 0)
        split_tensor(result, bits[0] & 1, send, keep)

    return body


def attend(bits, lengths, pieces, gain, bias, qkv_t, qv_bias, proj_w):
    parts = len(pieces)
    blk, t = pieces[0].shape
    d = parts * blk
    width = proj_w.shape[0]
    outs = [
        whole((parts // 2, blk, t), LOW), whole((parts // 2, blk, t), WIDE),
        whole((parts, blk, t), LOW), whole((d, t), LOW), whole((d, t), WIDE), whole((1, t), WIDE),
        whole((3 * width, t), LOW), whole((width, t), LOW), whole((width // HEAD_DIM, t), WIDE),
    ]
    return call(make_attend(parts), outs, [pltpu.VMEM((parts, blk, t), WIDE)], (bits, lengths),
                *pieces, gain, bias, qkv_t, qv_bias, proj_w)


def make_attend_back(parts):
    def body(bits, lengths, *refs):
        pieces = refs[:parts]
        (unit2, inverse2, gain2, cot, attended, qkv, totals, proj_w, normed, qkv_t, unit1,
         gain1, fc_b_grad, cot_sum) = refs[parts : parts + 14]
        (send, keep, first_send, first_keep, second_send, second_keep, mid_share, row_linear,
         small, full, result, grads, tokens_grad, square) = refs[parts + 14 :]
        assemble(bits, pieces, full)
        grad = flat(full).astype(WIDE)
        d, rows = grad.shape
        unit_v = unit2[...]
        along = grad * unit_v
        small[:, 0:d] = row_sums(along)
        small[:, d : 2 * d] = row_sums(grad)
        gain = column(gain2[...], rows)
        scaled = grad * gain
        mean = jnp.sum(scaled, axis=0, keepdims=True) / d
        slope = jnp.sum(along * gain, axis=0, keepdims=True) / d
        mid = cot[...].astype(WIDE) + inverse2[...] * (scaled - mean - unit_v * slope)
        small[:, 2 * d : 3 * d] = row_sums(mid)
        blk = result.shape[1]
        for j in range(parts):
            result[j] = mid[j * blk : (j + 1) * blk, :]
        mid_share[...] = result[bits[0]]
        tokens_grad[...] = mid.astype(LOW)
        width = proj_w.shape[0]
        half = square.shape[1]
        out_low = dot(proj_w[...], tokens_grad[...], 1, 0).astype(LOW)
        scale = HEAD_DIM ** (-0.5)
        heads = width // HEAD_DIM
        masks = [(at, key_range(at), allowed(lengths, at)) for at in range(0, rows, BLOCK)]
        for head in range(heads):
            here = head * HEAD_DIM
            dots = out_low[here : here + HEAD_DIM, :]
            row_dot = jnp.sum(
                dots.astype(WIDE) * attended[here : here + HEAD_DIM, :].astype(WIDE),
                axis=0, keepdims=True)
            k_sum = [None] * (rows // LANES)
            v_sum = [None] * (rows // LANES)
            for at, (low, high), mask in masks:
                q = qkv[here : here + HEAD_DIM, at : at + BLOCK]
                k = qkv[width + here : width + here + HEAD_DIM, low:high]
                v = qkv[2 * width + here : 2 * width + here + HEAD_DIM, low:high]
                da = dots[:, at : at + BLOCK]
                scores = jnp.where(mask, dot(k, q, 0, 0) * scale, MASKED)
                probs = jnp.exp(scores - totals[head : head + 1, at : at + BLOCK])
                weight_grad = dot(v, da, 0, 0)
                score = (probs * (weight_grad - row_dot[:, at : at + BLOCK]) * scale).astype(LOW)
                grads[here : here + HEAD_DIM, at : at + BLOCK] = dot(k, score, 1, 0).astype(LOW)
                k_part = dot(q, score, 1, 1)
                v_part = dot(da, probs.astype(LOW), 1, 1)
                for n in range((high - low) // LANES):
                    m = low // LANES + n
                    kp = k_part[:, n * LANES : (n + 1) * LANES]
                    vp = v_part[:, n * LANES : (n + 1) * LANES]
                    k_sum[m] = kp if k_sum[m] is None else k_sum[m] + kp
                    v_sum[m] = vp if v_sum[m] is None else v_sum[m] + vp
            for m in range(rows // LANES):
                sl = slice(m * LANES, (m + 1) * LANES)
                grads[width + here : width + here + HEAD_DIM, sl] = k_sum[m].astype(LOW)
                grads[2 * width + here : 2 * width + here + HEAD_DIM, sl] = v_sum[m].astype(LOW)
        made = dot(grads[0 : 2 * half, :], normed[...], 1, 1)
        for j in range(2):
            square[j] = made[j * half : (j + 1) * half, :]
        split_half(square, bits[1] & 1, first_send, first_keep)
        square[0] = dot(grads[2 * half : 3 * width, :], normed[...], 1, 1)
        square[1] = dot(attended[...], tokens_grad[...], 1, 1)
        split_half(square, (bits[1] >> 1) & 1, second_send, second_keep)
        sums = row_sums(grads[...].astype(WIDE))
        small[:, 3 * d : 3 * d + width] = sums[:, :width]
        small[:, 3 * d + width : 3 * d + 2 * width] = sums[:, 2 * width :]
        at = 3 * d + 2 * width
        small[:, at : at + d] = cot_sum[...]
        small[:, at + d :] = fc_b_grad[...]
        gain_first = column(gain1[...], rows)
        sum_rows = jnp.zeros((1, rows), WIDE)
        dot_rows = jnp.zeros((1, rows), WIDE)
        for j in range(parts):
            sl = slice(j * blk, (j + 1) * blk)
            part = dot(qkv_t[:, sl], grads[...], 0, 0)
            result[j] = part
            unit_part = unit1[sl, :]
            along = part * unit_part
            row_linear[:, 2 * rows + j * blk : 2 * rows + (j + 1) * blk] = row_sums(along)
            row_linear[:, 2 * rows + d + j * blk : 2 * rows + d + (j + 1) * blk] = row_sums(part)
            gain_part = gain_first[sl, :]
            sum_rows = sum_rows + jnp.sum(part * gain_part, axis=0, keepdims=True)
            dot_rows = dot_rows + jnp.sum(along * gain_part, axis=0, keepdims=True)
        row_linear[:, :rows] = sum_rows
        row_linear[:, rows : 2 * rows] = dot_rows
        split_tensor(result, bits[0] & 1, send, keep)

    return body


def attend_back(bits, lengths, pieces, unit2, inverse2, gain2, cot, attended, qkv, totals, proj_w,
                normed, qkv_t, unit1, gain1, fc_b_grad, cot_sum):
    parts = len(pieces)
    blk, t = pieces[0].shape
    d = parts * blk
    width = proj_w.shape[0]
    half = d // 4
    outs = [
        whole((parts // 2, blk, t), LOW), whole((parts // 2, blk, t), WIDE),
        whole((half, d), LOW), whole((half, d), WIDE), whole((half, d), LOW), whole((half, d), WIDE),
        whole((blk, t), WIDE), whole((1, 2 * t + 2 * d), WIDE), whole((1, 4 * d + 2 * width + fc_b_grad.shape[1]), WIDE),
    ]
    scratch = [pltpu.VMEM((parts, blk, t), LOW), pltpu.VMEM((parts, blk, t), WIDE),
               pltpu.VMEM((3 * width, t), LOW), pltpu.VMEM((d, t), LOW),
               pltpu.VMEM((2, half, d), WIDE)]
    return call(make_attend_back(parts), outs, scratch, (bits, lengths), *pieces, unit2, inverse2,
                gain2, cot, attended, qkv, totals, proj_w, normed, qkv_t, unit1, gain1,
                fc_b_grad, cot_sum)


def fold_body(bits, keep, other, send, kept, *, axis, bit):
    mine = (bits[axis] >> bit) & 1
    kept[...] = keep[mine] + other[mine].astype(WIDE)
    send[...] = (keep[1 - mine] + other[1 - mine].astype(WIDE)).astype(LOW)


def join_body(bits, block, other, out, *, axis, bit):
    mine = (bits[axis] >> bit) & 1
    out[mine] = block[...].astype(out.dtype)
    out[1 - mine] = other[...].astype(out.dtype)


def last_body(bits, first, first_other, second, second_other, qkv, proj):
    x_bit = bits[1] & 1
    z_bit = (bits[1] >> 1) & 1
    count = first.shape[0]
    qkv[pl.ds(pl.multiple_of(x_bit * count, count), count), :] = first[...].astype(WIDE)
    qkv[pl.ds(pl.multiple_of((1 - x_bit) * count, count), count), :] = first_other[...].astype(WIDE)
    mine = second[...].astype(WIDE)
    other = second_other[...].astype(WIDE)
    qkv[2 * count :, :] = jnp.where(z_bit == 1, other, mine)
    proj[...] = jnp.where(z_bit == 1, mine, other)


def tokens_body(bits, keep, other, mid_share, unit, inverse, gain, linear, out, turned):
    count, rows = keep.shape
    width = unit.shape[0]
    turned[...] = column(gain[...], LANES)
    at = pl.ds(pl.multiple_of(bits[0] * count, count), count)
    gain_v = jnp.concatenate([turned[at, :]] * (rows // LANES), axis=1)
    share = keep[...] + other[...].astype(WIDE)
    mean = linear[:, :rows] / width
    slope = linear[:, rows : 2 * rows] / width
    out[...] = mid_share[...] + inverse[...] * (share * gain_v - mean - unit[at, :] * slope)


AXES = ("tensor", "dp")


def make_local(sizes):
    tensor_bits = sizes["tensor"].bit_length() - 1
    dp_bits = sizes["dp"].bit_length() - 1
    order_one = list(range(dp_bits))
    order_two = [1, 0] + order_one[2:]

    def swap(value, axis, bit):
        return lax.ppermute(value, axis, [(i, i ^ (1 << bit)) for i in range(sizes[axis])])

    def gather(own):
        got = {0: own}
        for bit in reversed(range(tensor_bits)):
            for k in list(got):
                got[k | (1 << bit)] = swap(got[k], "tensor", bit)
        return [got[k] for k in sorted(got)]

    def local(tokens, lengths, ln1_gain, ln1_bias, qkv_weight, qv_bias, proj_weight, proj_bias,
              ln2_gain, ln2_bias, fc_weight, fc_bias, out_weight, out_bias, cotangent):
        place = [lax.axis_index("tensor"), lax.axis_index("dp")]
        bits = jnp.stack(place).astype(jnp.int32)
        width = proj_weight.shape[1]
        own_width = proj_weight.shape[0]
        row_count = tokens.shape[0]

        def fold(keep, other, axis, bit):
            shape = keep.shape[1:]
            if shape[0] % 16 == 0:
                return call(functools.partial(fold_body, axis=AXES.index(axis), bit=bit),
                            [whole(shape, LOW), whole(shape, WIDE)], [], (bits,), keep, other)
            total = keep + other.astype(WIDE)
            mine = (place[AXES.index(axis)] >> bit) & 1
            return (lax.dynamic_index_in_dim(total, 1 - mine, 0, False).astype(LOW),
                    lax.dynamic_index_in_dim(total, mine, 0, False))

        def join(block, other, axis, bit, dtype):
            count, cols = block.shape
            if count % 16 == 0:
                out = call(functools.partial(join_body, axis=AXES.index(axis), bit=bit),
                           [whole((2, count, cols), dtype)], [], (bits,), block, other)[0]
                return out.reshape(2 * count, cols)
            mine = (place[AXES.index(axis)] >> bit) & 1
            first = jnp.where(mine == 1, other, block)
            second = jnp.where(mine == 1, block, other)
            return jnp.concatenate([first, second]).astype(dtype)

        def halves(value):
            return value.reshape(2, value.shape[0] // 2, value.shape[1])

        def scatter_first(send, keep):
            other = swap(send, "tensor", 0)
            send, keep = fold(keep, other, "tensor", 1)
            return keep, swap(send, "tensor", 1)

        def sum_dp(send, keep, order):
            for bit in order[1:]:
                other = swap(send, "dp", order[order.index(bit) - 1])
                send, keep = fold(halves(keep), halves(other), "dp", bit)
            block = (keep + swap(send, "dp", order[-1]).astype(WIDE)).astype(LOW)
            for bit in reversed(order[1:]):
                block = join(block, swap(block, "dp", bit), "dp", bit, LOW)
            return block, swap(block, "dp", order[0])

        def row(vector):
            return vector.reshape(1, -1)

        qkv_t = jnp.swapaxes(qkv_weight, 1, 2).reshape(3 * own_width, width)
        gain1, gain2 = row(ln1_gain), row(ln2_gain)
        token_pieces = gather(tokens.T)
        cot_pieces = gather(cotangent.T)
        (send, keep, tokens_all, normed_one, unit_one, inverse_one, qkv, attended,
         totals) = attend(bits, lengths, token_pieces, gain1, row(ln1_bias), qkv_t, row(qv_bias),
                          proj_weight)
        keep, other = scatter_first(send, keep)
        mixed = gather((keep + other.astype(WIDE)).astype(LOW))
        (send, keep, hidden, grad_low, normed_two, unit_two, inverse_two, fc_b_grad, cot,
         base) = mlp(bits, mixed, cot_pieces, tokens_all.reshape(width, row_count), row(proj_bias),
                     gain2, row(ln2_bias), fc_weight, row(fc_bias), out_weight, row(out_bias))
        cot = cot.reshape(width, row_count)
        (out_send, out_keep, fc_send, fc_keep, mlp_send, mlp_keep, cot_sum) = mlp_grad(
            bits, hidden, grad_low, normed_two, out_weight, cot, sizes["tensor"])
        keep, other = scatter_first(send, keep)
        two_grad = gather((keep + other.astype(WIDE)).astype(LOW))
        out_mine, out_other = sum_dp(out_send, out_keep, order_one)
        fc_mine, fc_other = sum_dp(fc_send, fc_keep, order_two)
        grad_out_weight = join(out_mine, out_other, "dp", order_one[0], WIDE)
        grad_fc_weight = join(fc_mine, fc_other, "dp", order_two[0], WIDE)
        mlp_keep, mlp_other = scatter_first(mlp_send, mlp_keep)
        block_out = (base + (mlp_keep + mlp_other.astype(WIDE))).astype(LOW)
        (send, keep, first_send, first_keep, second_send, second_keep, mid_share, linear,
         small) = attend_back(bits, lengths, two_grad, unit_two, inverse_two, gain2, cot, attended,
                              qkv, totals, proj_weight, normed_one, qkv_t, unit_one, gain1,
                              fc_b_grad, cot_sum)
        for bit in range(tensor_bits):
            linear = linear + swap(linear, "tensor", bit)
        first, first_other = sum_dp(first_send, first_keep, order_one)
        second, second_other = sum_dp(second_send, second_keep, order_two)
        keep, other = scatter_first(send, keep)
        grad_tokens = call(tokens_body, [whole((own_width, row_count), WIDE)],
                           [pltpu.VMEM((width, LANES), WIDE)], (bits,), keep, other, mid_share,
                           unit_one, inverse_one, gain1, linear)[0]
        small = jnp.concatenate([small, linear[:, 2 * row_count :]], axis=1)
        for bit in range(dp_bits):
            small = small + swap(small, "dp", bit)
        grad_qkv, grad_proj_weight = call(
            last_body, [whole((3 * own_width, width), WIDE), whole((own_width, width), WIDE)], [],
            (bits,), first, first_other, second, second_other)
        grad_qkv_weight = jnp.swapaxes(grad_qkv.reshape(3, own_width, width), 1, 2)
        cuts = []
        at = 0
        for length in (width, width, width, 2 * own_width, width, fc_bias.shape[0], width, width):
            cuts.append(small[0, at : at + length])
            at += length
        return (
            block_out.T,
            grad_tokens.T,
            cuts[6],
            cuts[7],
            grad_qkv_weight,
            cuts[3].reshape(2, own_width),
            grad_proj_weight,
            cuts[2],
            cuts[0],
            cuts[1],
            grad_fc_weight,
            cuts[5],
            grad_out_weight,
            cuts[4],
        )

    return local


def solution(mesh):
    placed = (
        P("dp", "tensor"), P("dp", None), P(), P(), P(None, None, "tensor"), P(None, "tensor"),
        P("tensor", None), P(), P(), P(), P(None, "tensor"), P("tensor"), P("tensor", None), P(),
        P("dp", "tensor"),
    )
    given = (
        P("dp", "tensor"), P("dp", "tensor"), P(), P(), P(None, None, "tensor"),
        P(None, "tensor"), P("tensor", None), P(), P(), P(), P(None, "tensor"), P("tensor"),
        P("tensor", None), P(),
    )
    return jax.shard_map(
        make_local({axis: mesh.shape[axis] for axis in AXES}),
        mesh=mesh, in_specs=placed, out_specs=given, check_vma=False,
    )
```
